32 devices in a mesh: col: 4 (over y, x), bulk: 8 (over z, core).
Axes of the slice: x: 2, y: 2, z: 4, core: 2. Of those that a mesh axis runs over, the one named last changes fastest.
Arguments:
- sequence_embedding: bfloat16 [64, 128, 64], P('bulk', 'col'), may hold values from -6 to 6
- residue_couplings: bfloat16 [128, 128, 128], P('bulk', 'col'), may hold values from -6 to 6
- sequence_layernorm_factor: float32 [64], replicated, may hold values from 0.5 to 1.5
- coupling_layernorm_factor: float32 [128], replicated, may hold values from 0.5 to 1.5
- content_projection: bfloat16 [64, 256], replicated, may hold values from -0.75 to 0.75
- switch_projection: bfloat16 [64, 256], replicated, may hold values from -0.75 to 0.75
- attention_score_projection: bfloat16 [128, 8], replicated, may hold values from -0.29882812 to 0.29882812
- final_projection: bfloat16 [256, 64], replicated, may hold values from -2 to 2
- residual_change_cotangent: bfloat16 [64, 128, 64], P('bulk', 'col'), may hold values from -6 to 6
Outputs:
- residual_change: bfloat16 [64, 128, 64], P('bulk', 'col')
- sequence_embedding_sensitivity: bfloat16 [64, 128, 64], P('bulk', 'col')
- coupling_sensitivity: bfloat16 [128, 128, 128], P('bulk', 'col')
The draws below stay inside these ranges and needn't reach their ends.
All inputs are finite; a program needn't handle non-finite values.
Results may differ from the reference program's by a relative error of at most 0.025.
Values may be sent and summed in bfloat16 or wider, within the bound.
A program may use at most 64 MiB of HBM per device.

```python
import jax
import jax.numpy as jnp
from jax import lax

FEATURE_DEPTH = 64
CZ = 128
ATTENTION_SPLITS = 8
SPLIT_WIDTH = 32
TOKENS_PER_COL = 32
RESIDUE_COUNT = 128
SEQUENCE_COUNT = 64
N_COL = 4
N_BULK = 8


def shard_levels(own_key, extent, shards, smallest, largest):
    def one(position, shards_of):
        steps = jax.random.uniform(jax.random.fold_in(jax.random.fold_in(own_key, 6), position), (shards_of,), jnp.float32, smallest / len(shards), largest / len(shards))
        return jnp.repeat(jnp.exp(steps), extent[position] // shards_of).reshape((-1,) + (1,) * (len(extent) - position - 1))

    factor_of = one(*shards[0])
    for cut in shards[1:]:
        factor_of = factor_of * one(*cut)
    return factor_of


def centred(stream_key, dims, deviation, most, cuts=(), dtype=jnp.bfloat16):
    level = shard_levels(stream_key, dims, cuts, -0.22, 0.18) if cuts else 1.0
    result = jax.random.normal(stream_key, dims, jnp.float32) * deviation * level
    return jnp.minimum(jnp.maximum(result, -most), most).astype(dtype)


def setup_inputs(seed: int = 0) -> dict:
    key_list = jax.random.split(jax.random.key(seed), 10)
    return {
        "sequence_embedding": centred(key_list[0], (SEQUENCE_COUNT, RESIDUE_COUNT, FEATURE_DEPTH), 1.0, 6.0, ((0, 8), (1, 4))),
        "residue_couplings": centred(key_list[1], (RESIDUE_COUNT, RESIDUE_COUNT, CZ), 1.0, 6.0, ((0, 8), (1, 4))),
        "sequence_layernorm_factor": jnp.clip(1.0 + 0.1 * jax.random.normal(key_list[2], (FEATURE_DEPTH,), jnp.float32), 0.5, 1.5),
        "coupling_layernorm_factor": jnp.clip(1.0 + 0.1 * jax.random.normal(key_list[3], (CZ,), jnp.float32), 0.5, 1.5),
        "content_projection": centred(key_list[4], (FEATURE_DEPTH, ATTENTION_SPLITS * SPLIT_WIDTH), FEATURE_DEPTH ** -0.5, 0.75),
        "switch_projection": centred(key_list[5], (FEATURE_DEPTH, ATTENTION_SPLITS * SPLIT_WIDTH), FEATURE_DEPTH ** -0.5, 0.75),
        "attention_score_projection": jnp.clip(jax.random.uniform(key_list[6], (CZ, ATTENTION_SPLITS), jnp.float32, -0.29882812, 0.29882812), -0.29882812, 0.29882812).astype(jnp.bfloat16),
        "final_projection": centred(key_list[7], (ATTENTION_SPLITS * SPLIT_WIDTH, FEATURE_DEPTH), (max(SPLIT_WIDTH // 4, 1)) ** -0.5, 2.0),
        "residual_change_cotangent": centred(key_list[8], (SEQUENCE_COUNT, RESIDUE_COUNT, FEATURE_DEPTH), 1.0, 6.0, ((0, 8), (1, 4))),
    }


epsilon = 1e-05

def centred_sequences(inputs, scale_gain):
    widened = inputs.astype(jnp.float32)
    row_mean = lax.optimization_barrier(jnp.mean(widened, axis=-1, keepdims=True))
    centered = widened - row_mean
    variance = lax.optimization_barrier(jnp.mean(centered * centered, axis=-1, keepdims=True))
    inv_std = lax.rsqrt(variance + epsilon)
    normed = centered * inv_std
    return (normed * scale_gain, normed, inv_std)

def layernorm_reverse_mode(upstream, normed, inv_std, scale_gain):
    scaled = upstream * scale_gain
    mean_grad = lax.optimization_barrier(jnp.mean(scaled, axis=-1, keepdims=True))
    mean_proj = lax.optimization_barrier(jnp.mean(scaled * normed, axis=-1, keepdims=True))
    return inv_std * (scaled - mean_grad - normed * mean_proj)

def reference(sequence_embedding, residue_couplings, sequence_layernorm_factor, coupling_layernorm_factor, content_projection, switch_projection, attention_score_projection, final_projection, residual_change_cotangent):
    number_of_heads = attention_score_projection.shape[1]
    value_channels = content_projection.shape[1]
    head_channels = value_channels // number_of_heads
    pair_rows = RESIDUE_COUNT // N_BULK
    rows_per_group = SEQUENCE_COUNT // N_BULK
    channels = residue_couplings.shape[2]
    finest_accuracy = lax.Precision.HIGHEST
    out_wide = final_projection.astype(jnp.float32)
    switch_single_form = switch_projection.astype(jnp.float32)
    bias_wide = attention_score_projection.astype(jnp.float32)
    sequence_scaled_by_factor, sequence_centred_unit, sequence_reciprocal_spread = centred_sequences(sequence_embedding, sequence_layernorm_factor)
    sequence_embedding_brief = sequence_scaled_by_factor.astype(jnp.bfloat16)
    content_sequences = jnp.dot(sequence_embedding_brief, content_projection, preferred_element_type=jnp.float32).astype(jnp.bfloat16)
    sigmoid_switch = jax.nn.sigmoid(jnp.dot(sequence_embedding_brief, switch_projection, preferred_element_type=jnp.float32))
    pair_blocks = residue_couplings.reshape(N_BULK, pair_rows, RESIDUE_COUNT, channels)

    def block_logits(pair_block):
        scaled, _, _ = centred_sequences(pair_block, coupling_layernorm_factor)
        return jnp.einsum('ijk,kh->hij', scaled.astype(jnp.bfloat16).astype(jnp.float32), bias_wide)
    logits = lax.map(block_logits, pair_blocks)
    logits = jnp.transpose(logits, (1, 0, 2, 3)).reshape(number_of_heads, RESIDUE_COUNT, RESIDUE_COUNT)
    exponent = jnp.exp(logits)
    weights = exponent / lax.optimization_barrier(jnp.sum(exponent, axis=2, keepdims=True))
    weights_wide = weights.astype(jnp.bfloat16).astype(jnp.float32)
    value_per_head = content_sequences.astype(jnp.float32).reshape(SEQUENCE_COUNT, RESIDUE_COUNT, number_of_heads, head_channels)
    weight_cols = jnp.transpose(weights_wide.reshape(number_of_heads, RESIDUE_COUNT, N_COL, TOKENS_PER_COL), (2, 0, 1, 3))
    value_columns = jnp.transpose(value_per_head.reshape(SEQUENCE_COUNT, N_COL, TOKENS_PER_COL, number_of_heads, head_channels), (1, 0, 2, 3, 4))

    def add_cols(running, col_items):
        col_part = jnp.einsum('hit,sthc->sihc', col_items[0], col_items[1])
        rounded = lax.optimization_barrier(col_part.astype(jnp.bfloat16))
        return (running + rounded.astype(jnp.float32), None)
    average_start = jnp.zeros((SEQUENCE_COUNT, RESIDUE_COUNT, number_of_heads, head_channels), jnp.float32)
    pair_average, _ = lax.scan(add_cols, average_start, (weight_cols, value_columns))
    pair_average = pair_average.reshape(SEQUENCE_COUNT, RESIDUE_COUNT, value_channels)
    residual_change = jnp.dot(sigmoid_switch * pair_average, out_wide, precision=finest_accuracy).astype(jnp.bfloat16)
    d_gated = jnp.dot(residual_change_cotangent.astype(jnp.float32), out_wide.T, precision=finest_accuracy)
    average_gradient = (sigmoid_switch * d_gated).astype(jnp.bfloat16)
    switch_preimage_sensitivity = d_gated * pair_average * sigmoid_switch * (1.0 - sigmoid_switch)
    head_gradient = average_gradient.astype(jnp.float32).reshape(SEQUENCE_COUNT, RESIDUE_COUNT, number_of_heads, head_channels)
    content_sensitivity = jnp.einsum('hij,sihc->sjhc', weights_wide, head_gradient)
    content_sensitivity = content_sensitivity.reshape(SEQUENCE_COUNT, RESIDUE_COUNT, value_channels).astype(jnp.bfloat16)
    grad_groups = head_gradient.reshape(N_BULK, rows_per_group, RESIDUE_COUNT, number_of_heads, head_channels)
    value_groups = value_per_head.reshape(N_BULK, rows_per_group, RESIDUE_COUNT, number_of_heads, head_channels)

    def add_group(running, group_items):
        group_part = jnp.einsum('sihc,sjhc->hij', group_items[0], group_items[1])
        rounded = lax.optimization_barrier(group_part.astype(jnp.bfloat16))
        return (running + rounded.astype(jnp.float32), None)
    start_sum = jnp.zeros((number_of_heads, RESIDUE_COUNT, RESIDUE_COUNT), jnp.float32)
    d_weights, _ = lax.scan(add_group, start_sum, (grad_groups, value_groups))
    row_dot = lax.optimization_barrier(jnp.sum(weights_wide * d_weights, axis=2, keepdims=True))
    d_logits = weights * (d_weights - row_dot)
    logit_blocks = jnp.transpose(d_logits.reshape(number_of_heads, N_BULK, pair_rows, RESIDUE_COUNT), (1, 0, 2, 3))

    def block_grad(block_items):
        _, normed, inv_std = centred_sequences(block_items[0], coupling_layernorm_factor)
        d_normed = jnp.einsum('hij,kh->ijk', block_items[1], bias_wide, precision=finest_accuracy)
        return layernorm_reverse_mode(d_normed, normed, inv_std, coupling_layernorm_factor).astype(jnp.bfloat16)
    coupling_sensitivity = lax.map(block_grad, (pair_blocks, logit_blocks)).reshape(RESIDUE_COUNT, RESIDUE_COUNT, channels)
    sequence_sensitivity_brief = jnp.dot(content_sensitivity, content_projection.T, preferred_element_type=jnp.float32)
    sequence_sensitivity_brief = sequence_sensitivity_brief + jnp.dot(switch_preimage_sensitivity, switch_single_form.T, precision=finest_accuracy)
    sequence_embedding_sensitivity = layernorm_reverse_mode(sequence_sensitivity_brief, sequence_centred_unit, sequence_reciprocal_spread, sequence_layernorm_factor).astype(jnp.bfloat16)
    return (residual_change, sequence_embedding_sensitivity, coupling_sensitivity)
```

```python
import functools

import jax
import jax.numpy as jnp
from jax import lax
from jax.experimental import pallas as pl
from jax.experimental.pallas import tpu as pltpu
from jax.sharding import PartitionSpec as P

EPS = 1e-05
LANES = 128
MESH = pl.DeviceIdType.MESH
f32 = jnp.float32
bf16 = jnp.bfloat16


def dot(a, b):
    return jnp.dot(a, b, preferred_element_type=f32)


def dot_nt(a, b):
    return lax.dot_general(a, b, (((1,), (1,)), ((), ())), preferred_element_type=f32)


def dot_tn(a, b):
    return lax.dot_general(a, b, (((0,), (0,)), ((), ())), preferred_element_type=f32)


def normed_rows(x):
    centered = x - jnp.mean(x, axis=-1, keepdims=True)
    inv = lax.rsqrt(jnp.mean(centered * centered, axis=-1, keepdims=True) + EPS)
    return centered * inv, inv


def rows_backward(up, hat, inv, gain):
    q = up * gain
    mean_q = jnp.mean(q, axis=-1, keepdims=True)
    mean_p = jnp.mean(q * hat, axis=-1, keepdims=True)
    return inv * (q - mean_q - hat * mean_p)


def split_dot(a, b):
    high = a.astype(bf16)
    low = (a - high.astype(f32)).astype(bf16)
    return dot(high, b) + dot(low, b)


def loop(n, body):
    if n <= 8:
        for k in range(n):
            body(k)
    else:
        lax.fori_loop(0, n, lambda k, _: (body(k), 0)[1], 0)


def kernel(
    nc, nb, ns, nt, ni, nh,
    msa_ref, pair_ref, mgain_ref, pgain_ref, wv_ref, wg_ref, att_ref, wo_ref, cot_ref,
    res_ref, dmsa_ref, dpair_ref,
    x_all, e_all, bd, da, gate_s, dg_s, dw_s, inv_t, avg_s, dv_s, hat_s, rinv_s,
    phat_s, prinv_s, wvg, wop, rep, e_own, d_send, d_recv,
    xs_sem, xr_sem, es_sem, er_sem, ds_sem, dr_sem,
):
    c = lax.axis_index("col")
    b = lax.axis_index("bulk")
    depth = msa_ref.shape[1]
    chans = wv_ref.shape[1]
    tiles = chans // LANES
    hd = chans // nh
    per = LANES // hd
    n = nc * nt

    barrier = pltpu.get_barrier_semaphore()

    def greet(k, _):
        c2 = lax.rem(c + lax.div(k, nb), nc)
        b2 = lax.rem(b + lax.rem(k, nb), nb)
        pl.semaphore_signal(barrier, inc=1, device_id=(c2, b2), device_id_type=MESH)
        return 0

    lax.fori_loop(1, nc * nb, greet, 0)

    mgain = mgain_ref[...]
    pgain = pgain_ref[...]
    hat, rinv = normed_rows(msa_ref[...].astype(f32))
    hat_s[...] = hat
    rinv_s[...] = rinv
    x_all[c, :, :depth] = (hat * mgain).astype(bf16)
    x_all[c, :, depth:] = cot_ref[...]

    pl.semaphore_wait(barrier, nc * nb - 1)

    def x_copy(k):
        c2 = lax.rem(c + k, nc)
        return pltpu.make_async_remote_copy(
            src_ref=x_all.at[c], dst_ref=x_all.at[c],
            send_sem=xs_sem.at[k], recv_sem=xr_sem.at[c],
            device_id=(c2, b), device_id_type=MESH,
        )

    loop(nc - 1, lambda k: x_copy(k + 1).start())

    lane = lax.broadcasted_iota(jnp.int32, (nt, chans), 1)
    row = lax.broadcasted_iota(jnp.int32, (nt, chans), 0)
    same_j = (lax.rem(lane, nt) == row).astype(f32)
    spread = (
        lax.div(lax.broadcasted_iota(jnp.int32, (nh, chans), 1), nt)
        == lax.broadcasted_iota(jnp.int32, (nh, chans), 0)
    ).astype(bf16)
    rep[...] = dot(att_ref[...], spread).astype(bf16)
    phat, prinv = normed_rows(pair_ref[...].astype(f32))
    phat_s[...] = phat
    prinv_s[...] = prinv
    many = dot((phat * pgain).astype(bf16), rep[...])
    logits = jnp.sum(many.reshape(ni, nt, chans) * same_j[None], axis=1)
    e = jnp.exp(logits)
    e_own[...] = e
    my_rows = pl.ds(pl.multiple_of(b * ni, ni), ni)
    e_all[c, my_rows, :] = e.astype(bf16)

    def e_copy(k, send):
        c2 = lax.rem(c + lax.div(k, nb), nc)
        b2 = lax.rem(b + lax.rem(k, nb), nb)
        if send:
            block = e_all.at[c, my_rows]
            slot = er_sem.at[c * nb + b]
        else:
            block = e_all.at[c2, pl.ds(pl.multiple_of(b2 * ni, ni), ni)]
            slot = er_sem.at[c2 * nb + b2]
        return pltpu.make_async_remote_copy(
            src_ref=block, dst_ref=block, send_sem=es_sem.at[k], recv_sem=slot,
            device_id=(c2, b2), device_id_type=MESH,
        )

    def e_start(k, _):
        e_copy(k, True).start()
        return 0

    lax.fori_loop(1, nc * nb, e_start, 0)

    wvg[:depth, :chans] = wv_ref[...]
    wvg[:depth, chans:] = wg_ref[...]
    wvg[depth:, :] = jnp.zeros((depth, 2 * chans), bf16)
    wop[:, :depth] = jnp.zeros((chans, depth), bf16)
    wop[:, depth:] = wo_ref[...]

    head_of = lax.div(lax.broadcasted_iota(jnp.int32, (nt, LANES), 1), hd)
    head_masks = [(head_of == h).astype(f32).astype(bf16) for h in range(per)]

    def chunk(k):
        c2 = lax.rem(c + k, nc)
        if not (isinstance(k, int) and k == 0):
            block = x_all.at[c2]
            pltpu.make_async_remote_copy(
                src_ref=block, dst_ref=block, send_sem=xs_sem.at[k], recv_sem=xr_sem.at[c2],
                device_id=(c2, b), device_id_type=MESH,
            ).wait_recv()
        x = x_all[c2]
        both = dot(x, wvg[...])
        values = both[:, :chans].astype(bf16)
        gate = 1.0 / (1.0 + jnp.exp(-both[:, chans:]))
        dg = dot_nt(x, wop[...])
        dav = (gate * dg).astype(bf16)
        if isinstance(k, int) and k == 0:
            gate_s[...] = gate
            dg_s[...] = dg
        rows = pl.ds(pl.multiple_of(c2 * nt, nt), nt)
        for s in range(ns):
            for t in range(tiles):
                cut = (slice(s * nt, (s + 1) * nt), slice(t * LANES, (t + 1) * LANES))
                da[t, rows, s * LANES:(s + 1) * LANES] = dav[cut]
                piece = values[cut]
                for h in range(per):
                    bd[c2, t, h * nt:(h + 1) * nt, s * LANES:(s + 1) * LANES] = piece * head_masks[h]

    chunk(0)
    loop(nc - 1, lambda k: chunk(k + 1))

    def e_wait(k, _):
        e_copy(k, False).wait_recv()
        return 0

    lax.fori_loop(1, nc * nb, e_wait, 0)

    group = (
        lax.div(lax.broadcasted_iota(jnp.int32, (LANES, LANES), 1), hd)
        == lax.div(lax.broadcasted_iota(jnp.int32, (LANES, LANES), 0), hd)
    ).astype(f32).astype(bf16)
    for t in range(tiles):
        lanes = slice(t * LANES, (t + 1) * LANES)

        def term(c2):
            grad = dot_nt(da[t], bd[c2, t])
            weight = e_all[c2, :, lanes].astype(f32)
            return grad, weight * grad, weight

        own, dot_sum, e_sum = term(c)
        dw_s[...] = own

        def more(k, carry):
            _, x, y = term(lax.rem(c + k, nc))
            return carry[0] + x, carry[1] + y

        if nc <= 4:
            for k in range(1, nc):
                dot_sum, e_sum = more(k, (dot_sum, e_sum))
        else:
            dot_sum, e_sum = lax.fori_loop(1, nc, more, (dot_sum, e_sum))
        inverse = 1.0 / split_dot(e_sum, group)
        inv_t[:, lanes] = inverse
        diff = dw_s[...] - split_dot(dot_sum, group) * inverse
        d_send[:, :, lanes] = diff.astype(bf16).reshape(nb, ni, LANES)

    def d_copy(k, send):
        b2 = lax.rem(b + k, nb)
        return pltpu.make_async_remote_copy(
            src_ref=d_send.at[b2], dst_ref=d_recv.at[b if send else b2],
            send_sem=ds_sem.at[k], recv_sem=dr_sem.at[b if send else b2],
            device_id=(c, b2), device_id_type=MESH,
        )

    loop(nb - 1, lambda k: d_copy(k + 1, True).start())

    tokens = pl.ds(pl.multiple_of(c * nt, nt), nt)
    for t in range(tiles):
        lanes = slice(t * LANES, (t + 1) * LANES)
        scale = inv_t[tokens, lanes]

        def add(k, total):
            return total + dot(e_all[k, tokens, lanes], bd[k, t])

        total = jnp.zeros((nt, ns * LANES), f32)
        if nc <= 4:
            for k in range(nc):
                total = add(k, total)
        else:
            total = lax.fori_loop(0, nc, add, total)
        weight = (e_all[c, :, lanes].astype(f32) * inv_t[:, lanes]).astype(bf16)
        back = dot_tn(weight, da[t])
        for s in range(ns):
            span = slice(s * LANES, (s + 1) * LANES)
            avg_s[s * nt:(s + 1) * nt, lanes] = total[:, span] * scale
            picked = back[:nt, span]
            for h in range(1, per):
                picked = jnp.where(head_of == h, back[h * nt:(h + 1) * nt, span], picked)
            dv_s[s * nt:(s + 1) * nt, lanes] = picked.astype(bf16)
    gate = gate_s[...]
    gated = gate * avg_s[...]
    res_ref[...] = dot(gated.astype(bf16), wo_ref[...]).astype(bf16)
    d_pre = dg_s[...] * gated * (1.0 - gate)
    d_low = dot_nt(dv_s[...], wv_ref[...]) + dot_nt(d_pre.astype(bf16), wg_ref[...])
    dmsa_ref[...] = rows_backward(d_low, hat_s[...], rinv_s[...], mgain).astype(bf16)

    coeff = e_own[...] * inv_t[my_rows, :]
    total = d_send[b].astype(f32)
    for k in range(1, nb):
        d_copy(k, False).wait_recv()
        total = total + d_recv[lax.rem(b + k, nb)].astype(f32)
    d_logits = coeff * total
    wide = (d_logits[:, None, :] * same_j[None]).astype(bf16).reshape(ni * nt, chans)
    d_pair = dot_nt(wide, rep[...])
    dpair_ref[...] = rows_backward(d_pair, phat_s[...], prinv_s[...], pgain).astype(bf16)

    loop(nc - 1, lambda k: x_copy(k + 1).wait_send())

    def e_sent(k, _):
        e_copy(k, True).wait_send()
        return 0

    lax.fori_loop(1, nc * nb, e_sent, 0)
    loop(nb - 1, lambda k: d_copy(k + 1, True).wait_send())


def per_device(nc, nb, msa, pair, mgain, pgain, wv, wg, att, wo, cot):
    ns, nt, depth = msa.shape
    ni, nj, cz = pair.shape
    chans = wv.shape[1]
    nh = att.shape[1]
    tiles = chans // LANES
    n = nc * nt
    assert chans // nh == nt == nj and n == nb * ni and 2 * depth == LANES == cz
    rows = ns * nt
    vmem = pl.BlockSpec(memory_space=pltpu.VMEM)
    dma = pltpu.SemaphoreType.DMA
    outs = pl.pallas_call(
        functools.partial(kernel, nc, nb, ns, nt, ni, nh),
        out_shape=(
            jax.ShapeDtypeStruct((rows, depth), bf16),
            jax.ShapeDtypeStruct((rows, depth), bf16),
            jax.ShapeDtypeStruct((ni * nj, cz), bf16),
        ),
        in_specs=[vmem] * 9,
        out_specs=(vmem,) * 3,
        scratch_shapes=[
            pltpu.VMEM((nc, rows, LANES), bf16),
            pltpu.VMEM((nc, n, chans), bf16),
            pltpu.VMEM((nc, tiles, LANES, ns * LANES), bf16),
            pltpu.VMEM((tiles, n, ns * LANES), bf16),
            pltpu.VMEM((rows, chans), f32),
            pltpu.VMEM((rows, chans), f32),
            pltpu.VMEM((n, LANES), f32),
            pltpu.VMEM((n, chans), f32),
            pltpu.VMEM((rows, chans), f32),
            pltpu.VMEM((rows, chans), bf16),
            pltpu.VMEM((rows, depth), f32),
            pltpu.VMEM((rows, 1), f32),
            pltpu.VMEM((ni * nj, cz), f32),
            pltpu.VMEM((ni * nj, 1), f32),
            pltpu.VMEM((LANES, 2 * chans), bf16),
            pltpu.VMEM((chans, LANES), bf16),
            pltpu.VMEM((cz, chans), bf16),
            pltpu.VMEM((ni, chans), f32),
            pltpu.VMEM((nb, ni, chans), bf16),
            pltpu.VMEM((nb, ni, chans), bf16),
            dma((nc,)), dma((nc,)), dma((nc * nb,)), dma((nc * nb,)), dma((nb,)), dma((nb,)),
        ],
        compiler_params=pltpu.CompilerParams(
            collective_id=0, has_side_effects=True, vmem_limit_bytes=60 * 1024 * 1024
        ),
    )(
        msa.reshape(rows, depth), pair.reshape(ni * nj, cz),
        mgain.reshape(1, depth), pgain.reshape(1, cz), wv, wg, att, wo,
        cot.reshape(rows, depth),
    )
    return outs[0].reshape(msa.shape), outs[1].reshape(msa.shape), outs[2].reshape(pair.shape)


def solution(mesh):
    block = P("bulk", "col", None)
    return jax.shard_map(
        functools.partial(per_device, mesh.shape["col"], mesh.shape["bulk"]),
        mesh=mesh,
        in_specs=(block, block, P(), P(), P(), P(), P(), P(), block),
        out_specs=(block, block, block),
        check_vma=False,
    )
```

```python
import functools

import jax
import jax.numpy as jnp
from jax import lax
from jax.experimental import pallas as pl
from jax.experimental.pallas import tpu as pltpu
from jax.sharding import PartitionSpec as P

EPS = 1e-05
LANES = 128
MESH = pl.DeviceIdType.MESH
f32 = jnp.float32
bf16 = jnp.bfloat16


def dot(a, b):
    return jnp.dot(a, b, preferred_element_type=f32)


def dot_nt(a, b):
    return lax.dot_general(a, b, (((1,), (1,)), ((), ())), preferred_element_type=f32)


def dot_tn(a, b):
    return lax.dot_general(a, b, (((0,), (0,)), ((), ())), preferred_element_type=f32)


def normed_rows(x):
    centered = x - jnp.mean(x, axis=-1, keepdims=True)
    inv = lax.rsqrt(jnp.mean(centered * centered, axis=-1, keepdims=True) + EPS)
    return centered * inv, inv


def rows_backward(up, hat, inv, gain):
    q = up * gain
    mean_q = jnp.mean(q, axis=-1, keepdims=True)
    mean_p = jnp.mean(q * hat, axis=-1, keepdims=True)
    return inv * (q - mean_q - hat * mean_p)


def split_dot(a, b):
    high = a.astype(bf16)
    low = (a - high.astype(f32)).astype(bf16)
    return dot(high, b) + dot(low, b)


def loop(n, body):
    if n <= 8:
        for k in range(n):
            body(k)
    else:
        lax.fori_loop(0, n, lambda k, _: (body(k), 0)[1], 0)


def kernel(
    nc, nb, ns, nt, ni, nh,
    msa_in, pair_in, mgain_in, pgain_in, wv_in, wg_in, att_in, wo_in, cot_in,
    res_ref, dmsa_ref, dpair_ref,
    x_all, e_all, bd, da, gate_s, dg_s, dw_s, inv_t, avg_s, dv_s, hat_s, rinv_s,
    phat_s, prinv_s, wvg, wop, rep, e_own, d_send, d_recv,
    msa_ref, pair_ref, mgain_ref, pgain_ref, wv_ref, wg_ref, att_ref, wo_ref, cot_ref,
    xs_sem, xr_sem, es_sem, er_sem, ds_sem, dr_sem, in_sem,
):
    c = lax.axis_index("col")
    b = lax.axis_index("bulk")
    depth = msa_ref.shape[1]
    chans = wv_ref.shape[1]
    tiles = chans // LANES
    hd = chans // nh
    per = LANES // hd
    n = nc * nt

    pairs = (
        (msa_in, msa_ref), (mgain_in, mgain_ref), (cot_in, cot_ref),
        (pair_in, pair_ref), (pgain_in, pgain_ref), (att_in, att_ref),
        (wv_in, wv_ref), (wg_in, wg_ref), (wo_in, wo_ref),
    )
    loads = [pltpu.make_async_copy(x, y, in_sem.at[k]) for k, (x, y) in enumerate(pairs)]
    for load in loads:
        load.start()

    barrier = pltpu.get_barrier_semaphore()

    def greet(k, _):
        c2 = lax.rem(c + lax.div(k, nb), nc)
        b2 = lax.rem(b + lax.rem(k, nb), nb)
        pl.semaphore_signal(barrier, inc=1, device_id=(c2, b2), device_id_type=MESH)
        return 0

    lax.fori_loop(1, nc * nb, greet, 0)

    for load in loads[:3]:
        load.wait()
    mgain = mgain_ref[...]
    hat, rinv = normed_rows(msa_ref[...].astype(f32))
    hat_s[...] = hat
    rinv_s[...] = rinv
    x_all[c, :, :depth] = (hat * mgain).astype(bf16)
    x_all[c, :, depth:] = cot_ref[...]

    pl.semaphore_wait(barrier, nc * nb - 1)

    def x_copy(k):
        c2 = lax.rem(c + k, nc)
        return pltpu.make_async_remote_copy(
            src_ref=x_all.at[c], dst_ref=x_all.at[c],
            send_sem=xs_sem.at[k], recv_sem=xr_sem.at[c],
            device_id=(c2, b), device_id_type=MESH,
        )

    loop(nc - 1, lambda k: x_copy(k + 1).start())

    lane = lax.broadcasted_iota(jnp.int32, (nt, chans), 1)
    row = lax.broadcasted_iota(jnp.int32, (nt, chans), 0)
    same_j = (lax.rem(lane, nt) == row).astype(f32)
    spread = (
        lax.div(lax.broadcasted_iota(jnp.int32, (nh, chans), 1), nt)
        == lax.broadcasted_iota(jnp.int32, (nh, chans), 0)
    ).astype(bf16)
    for load in loads[3:6]:
        load.wait()
    pgain = pgain_ref[...]
    rep[...] = dot_tn(att_ref[...], spread).astype(bf16)
    phat, prinv = normed_rows(pair_ref[...].astype(f32))
    phat_s[...] = phat
    prinv_s[...] = prinv
    many = dot((phat * pgain).astype(bf16), rep[...])
    logits = jnp.sum(many.reshape(ni, nt, chans) * same_j[None], axis=1)
    e = jnp.exp(logits)
    e_own[...] = e
    my_rows = pl.ds(pl.multiple_of(b * ni, ni), ni)
    e_all[c, my_rows, :] = e.astype(bf16)

    def e_copy(k, send):
        c2 = lax.rem(c + lax.div(k, nb), nc)
        b2 = lax.rem(b + lax.rem(k, nb), nb)
        if send:
            block = e_all.at[c, my_rows]
            slot = er_sem.at[c * nb + b]
        else:
            block = e_all.at[c2, pl.ds(pl.multiple_of(b2 * ni, ni), ni)]
            slot = er_sem.at[c2 * nb + b2]
        return pltpu.make_async_remote_copy(
            src_ref=block, dst_ref=block, send_sem=es_sem.at[k], recv_sem=slot,
            device_id=(c2, b2), device_id_type=MESH,
        )

    def e_start(k, _):
        e_copy(k, True).start()
        return 0

    lax.fori_loop(1, nc * nb, e_start, 0)

    for load in loads[6:]:
        load.wait()
    wvg[:depth, :chans] = wv_ref[...]
    wvg[:depth, chans:] = wg_ref[...]
    wvg[depth:, :] = jnp.zeros((depth, 2 * chans), bf16)
    wop[:depth, :] = jnp.zeros((depth, chans), bf16)
    wop[depth:, :] = wo_ref[...]

    head_of = lax.div(lax.broadcasted_iota(jnp.int32, (nt, LANES), 1), hd)
    head_masks = [(head_of == h).astype(f32).astype(bf16) for h in range(per)]

    def chunk(k):
        c2 = lax.rem(c + k, nc)
        if not (isinstance(k, int) and k == 0):
            block = x_all.at[c2]
            pltpu.make_async_remote_copy(
                src_ref=block, dst_ref=block, send_sem=xs_sem.at[k], recv_sem=xr_sem.at[c2],
                device_id=(c2, b), device_id_type=MESH,
            ).wait_recv()
        x = x_all[c2]
        both = dot(x, wvg[...])
        values = both[:, :chans].astype(bf16)
        gate = 1.0 / (1.0 + jnp.exp(-both[:, chans:]))
        dg = dot(x, wop[...])
        dav = (gate * dg).astype(bf16)
        if isinstance(k, int) and k == 0:
            gate_s[...] = gate
            dg_s[...] = dg
        rows = pl.ds(pl.multiple_of(c2 * nt, nt), nt)
        for s in range(ns):
            for t in range(tiles):
                cut = (slice(s * nt, (s + 1) * nt), slice(t * LANES, (t + 1) * LANES))
                da[t, rows, s * LANES:(s + 1) * LANES] = dav[cut]
                piece = values[cut]
                for h in range(per):
                    bd[c2, t, h * nt:(h + 1) * nt, s * LANES:(s + 1) * LANES] = piece * head_masks[h]

    chunk(0)
    loop(nc - 1, lambda k: chunk(k + 1))

    def e_wait(k, _):
        e_copy(k, False).wait_recv()
        return 0

    lax.fori_loop(1, nc * nb, e_wait, 0)

    group = (
        lax.div(lax.broadcasted_iota(jnp.int32, (LANES, LANES), 1), hd)
        == lax.div(lax.broadcasted_iota(jnp.int32, (LANES, LANES), 0), hd)
    ).astype(f32).astype(bf16)
    for t in range(tiles):
        lanes = slice(t * LANES, (t + 1) * LANES)

        def term(c2):
            grad = dot_nt(da[t], bd[c2, t])
            weight = e_all[c2, :, lanes].astype(f32)
            return grad, weight * grad, weight

        own, dot_sum, e_sum = term(c)
        dw_s[...] = own

        def more(k, carry):
            _, x, y = term(lax.rem(c + k, nc))
            return carry[0] + x, carry[1] + y

        if nc <= 4:
            for k in range(1, nc):
                dot_sum, e_sum = more(k, (dot_sum, e_sum))
        else:
            dot_sum, e_sum = lax.fori_loop(1, nc, more, (dot_sum, e_sum))
        inverse = 1.0 / split_dot(e_sum, group)
        inv_t[:, lanes] = inverse
        diff = dw_s[...] - split_dot(dot_sum, group) * inverse
        d_send[:, :, lanes] = diff.astype(bf16).reshape(nb, ni, LANES)

    def d_copy(k, send):
        b2 = lax.rem(b + k, nb)
        return pltpu.make_async_remote_copy(
            src_ref=d_send.at[b2], dst_ref=d_recv.at[b if send else b2],
            send_sem=ds_sem.at[k], recv_sem=dr_sem.at[b if send else b2],
            device_id=(c, b2), device_id_type=MESH,
        )

    loop(nb - 1, lambda k: d_copy(k + 1, True).start())

    tokens = pl.ds(pl.multiple_of(c * nt, nt), nt)
    for t in range(tiles):
        lanes = slice(t * LANES, (t + 1) * LANES)
        scale = inv_t[tokens, lanes]

        def add(k, total):
            return total + dot(e_all[k, tokens, lanes], bd[k, t])

        total = jnp.zeros((nt, ns * LANES), f32)
        if nc <= 4:
            for k in range(nc):
                total = add(k, total)
        else:
            total = lax.fori_loop(0, nc, add, total)
        weight = (e_all[c, :, lanes].astype(f32) * inv_t[:, lanes]).astype(bf16)
        back = dot_tn(weight, da[t])
        for s in range(ns):
            span = slice(s * LANES, (s + 1) * LANES)
            avg_s[s * nt:(s + 1) * nt, lanes] = total[:, span] * scale
            picked = back[:nt, span]
            for h in range(1, per):
                picked = jnp.where(head_of == h, back[h * nt:(h + 1) * nt, span], picked)
            dv_s[s * nt:(s + 1) * nt, lanes] = picked.astype(bf16)
    gate = gate_s[...]
    gated = gate * avg_s[...]
    res_ref[...] = dot_nt(gated.astype(bf16), wo_ref[...]).astype(bf16)
    d_pre = dg_s[...] * gated * (1.0 - gate)
    d_low = dot_nt(dv_s[...], wv_ref[...]) + dot_nt(d_pre.astype(bf16), wg_ref[...])
    dmsa_ref[...] = rows_backward(d_low, hat_s[...], rinv_s[...], mgain).astype(bf16)

    coeff = e_own[...] * inv_t[my_rows, :]
    total = d_send[b].astype(f32)
    for k in range(1, nb):
        d_copy(k, False).wait_recv()
        total = total + d_recv[lax.rem(b + k, nb)].astype(f32)
    d_logits = coeff * total
    wide = (d_logits[:, None, :] * same_j[None]).astype(bf16).reshape(ni * nt, chans)
    d_pair = dot_nt(wide, rep[...])
    dpair_ref[...] = rows_backward(d_pair, phat_s[...], prinv_s[...], pgain).astype(bf16)

    loop(nc - 1, lambda k: x_copy(k + 1).wait_send())

    def e_sent(k, _):
        e_copy(k, True).wait_send()
        return 0

    lax.fori_loop(1, nc * nb, e_sent, 0)
    loop(nb - 1, lambda k: d_copy(k + 1, True).wait_send())


def put_out(*refs):
    sems = refs[-1]
    copies = [pltpu.make_async_copy(refs[k], refs[k + 3], sems.at[k]) for k in range(3)]
    for copy in copies:
        copy.start()
    for copy in copies:
        copy.wait()


def per_device(nc, nb, msa, pair, mgain, pgain, wv, wg, att, wo, cot):
    ns, nt, depth = msa.shape
    ni, nj, cz = pair.shape
    chans = wv.shape[1]
    nh = att.shape[1]
    tiles = chans // LANES
    n = nc * nt
    assert chans // nh == nt == nj and n == nb * ni and 2 * depth == LANES == cz
    rows = ns * nt
    vmem = pl.BlockSpec(memory_space=pltpu.VMEM)
    dma = pltpu.SemaphoreType.DMA
    outs = pl.pallas_call(
        functools.partial(kernel, nc, nb, ns, nt, ni, nh),
        out_shape=(
            pltpu.VMEM((rows, depth), bf16),
            pltpu.VMEM((rows, depth), bf16),
            pltpu.VMEM((ni * nj, cz), bf16),
        ),
        in_specs=[pl.BlockSpec(memory_space=pltpu.HBM)] * 9,
        out_specs=(vmem,) * 3,
        scratch_shapes=[
            pltpu.VMEM((nc, rows, LANES), bf16),
            pltpu.VMEM((nc, n, chans), bf16),
            pltpu.VMEM((nc, tiles, LANES, ns * LANES), bf16),
            pltpu.VMEM((tiles, n, ns * LANES), bf16),
            pltpu.VMEM((rows, chans), f32),
            pltpu.VMEM((rows, chans), f32),
            pltpu.VMEM((n, LANES), f32),
            pltpu.VMEM((n, chans), f32),
            pltpu.VMEM((rows, chans), f32),
            pltpu.VMEM((rows, chans), bf16),
            pltpu.VMEM((rows, depth), f32),
            pltpu.VMEM((rows, 1), f32),
            pltpu.VMEM((ni * nj, cz), f32),
            pltpu.VMEM((ni * nj, 1), f32),
            pltpu.VMEM((LANES, 2 * chans), bf16),
            pltpu.VMEM((LANES, chans), bf16),
            pltpu.VMEM((cz, chans), bf16),
            pltpu.VMEM((ni, chans), f32),
            pltpu.VMEM((nb, ni, chans), bf16),
            pltpu.VMEM((nb, ni, chans), bf16),
            pltpu.VMEM((rows, depth), bf16),
            pltpu.VMEM((ni * nj, cz), bf16),
            pltpu.VMEM((1, depth), f32),
            pltpu.VMEM((1, cz), f32),
            pltpu.VMEM(wv.shape, bf16),
            pltpu.VMEM(wg.shape, bf16),
            pltpu.VMEM((nh, cz), bf16),
            pltpu.VMEM((depth, chans), bf16),
            pltpu.VMEM((rows, depth), bf16),
            dma((nc,)), dma((nc,)), dma((nc * nb,)), dma((nc * nb,)), dma((nb,)), dma((nb,)),
            dma((9,)),
        ],
        compiler_params=pltpu.CompilerParams(
            collective_id=0, has_side_effects=True, vmem_limit_bytes=62 * 1024 * 1024
        ),
    )(
        msa.reshape(rows, depth), pair.reshape(ni * nj, cz),
        mgain.reshape(1, depth), pgain.reshape(1, cz), wv, wg, att.T, wo.T,
        cot.reshape(rows, depth),
    )
    outs = pl.pallas_call(
        put_out,
        out_shape=tuple(jax.ShapeDtypeStruct(o.shape, o.dtype) for o in outs),
        in_specs=[vmem] * 3,
        out_specs=(pl.BlockSpec(memory_space=pltpu.HBM),) * 3,
        scratch_shapes=[dma((3,))],
        compiler_params=pltpu.CompilerParams(vmem_limit_bytes=4 * 1024 * 1024),
    )(*outs)
    return outs[0].reshape(msa.shape), outs[1].reshape(msa.shape), outs[2].reshape(pair.shape)


def solution(mesh):
    block = P("bulk", "col", None)
    return jax.shard_map(
        functools.partial(per_device, mesh.shape["col"], mesh.shape["bulk"]),
        mesh=mesh,
        in_specs=(block, block, P(), P(), P(), P(), P(), P(), block),
        out_specs=(block, block, block),
        check_vma=False,
    )
```

```python
import functools

import jax
import jax.numpy as jnp
from jax import lax
from jax.experimental import pallas as pl
from jax.experimental.pallas import tpu as pltpu
from jax.sharding import PartitionSpec as P

EPS = 1e-05
LANES = 128
MESH = pl.DeviceIdType.MESH
f32 = jnp.float32
bf16 = jnp.bfloat16


def dot(a, b):
    return jnp.dot(a, b, preferred_element_type=f32)


def dot_nt(a, b):
    return lax.dot_general(a, b, (((1,), (1,)), ((), ())), preferred_element_type=f32)


def dot_tn(a, b):
    return lax.dot_general(a, b, (((0,), (0,)), ((), ())), preferred_element_type=f32)


def normed_rows(x):
    centered = x - jnp.mean(x, axis=-1, keepdims=True)
    inv = lax.rsqrt(jnp.mean(centered * centered, axis=-1, keepdims=True) + EPS)
    return centered * inv, inv


def rows_backward(up, hat, inv, gain):
    q = up * gain
    mean_q = jnp.mean(q, axis=-1, keepdims=True)
    mean_p = jnp.mean(q * hat, axis=-1, keepdims=True)
    return inv * (q - mean_q - hat * mean_p)


def split_dot(a, b):
    high = a.astype(bf16)
    low = (a - high.astype(f32)).astype(bf16)
    return dot(high, b) + dot(low, b)


def loop(n, body):
    if n <= 8:
        for k in range(n):
            body(k)
    else:
        lax.fori_loop(0, n, lambda k, _: (body(k), 0)[1], 0)


def kernel(
    nc, nb, ns, nt, ni, nh,
    msa_in, pair_in, mgain_in, pgain_in, wv_in, wg_in, att_in, wo_in, cot_in,
    res_ref, dmsa_ref, dpair_ref,
    x_all, e_all, bd, da, gate_s, dg_s, dw_s, inv_t, avg_s, dv_s, hat_s, rinv_s,
    phat_s, prinv_s, wvg, wop, rep, e_own, d_send, d_recv,
    msa_ref, pair_ref, mgain_ref, pgain_ref, wv_ref, wg_ref, att_ref, wo_ref, cot_ref,
    xs_sem, xr_sem, es_sem, er_sem, ds_sem, dr_sem, in_sem,
):
    c = lax.axis_index("col")
    b = lax.axis_index("bulk")
    depth = msa_ref.shape[1]
    chans = wv_ref.shape[1]
    tiles = chans // LANES
    hd = chans // nh
    per = LANES // hd
    n = nc * nt

    pairs = (
        (msa_in, msa_ref), (mgain_in, mgain_ref), (cot_in, cot_ref),
        (pair_in, pair_ref), (pgain_in, pgain_ref), (att_in, att_ref),
        (wv_in, wv_ref), (wg_in, wg_ref), (wo_in, wo_ref),
    )
    loads = [pltpu.make_async_copy(x, y, in_sem.at[k]) for k, (x, y) in enumerate(pairs)]
    for load in loads:
        load.start()

    barrier = pltpu.get_barrier_semaphore()

    def greet(k, _):
        c2 = lax.rem(c + lax.div(k, nb), nc)
        b2 = lax.rem(b + lax.rem(k, nb), nb)
        pl.semaphore_signal(barrier, inc=1, device_id=(c2, b2), device_id_type=MESH)
        return 0

    lax.fori_loop(1, nc * nb, greet, 0)

    for load in loads[:3]:
        load.wait()
    mgain = mgain_ref[...]
    hat, rinv = normed_rows(msa_ref[...].astype(f32))
    hat_s[...] = hat
    rinv_s[...] = rinv
    x_all[c, :, :depth] = (hat * mgain).astype(bf16)
    x_all[c, :, depth:] = cot_ref[...]

    lane = lax.broadcasted_iota(jnp.int32, (nt, chans), 1)
    row = lax.broadcasted_iota(jnp.int32, (nt, chans), 0)
    same_j = (lax.rem(lane, nt) == row).astype(f32)
    spread = (
        lax.div(lax.broadcasted_iota(jnp.int32, (nh, chans), 1), nt)
        == lax.broadcasted_iota(jnp.int32, (nh, chans), 0)
    ).astype(bf16)
    for load in loads[3:6]:
        load.wait()
    pgain = pgain_ref[...]
    rep[...] = dot_tn(att_ref[...], spread).astype(bf16)
    phat, prinv = normed_rows(pair_ref[...].astype(f32))
    phat_s[...] = phat
    prinv_s[...] = prinv
    many = dot((phat * pgain).astype(bf16), rep[...])
    logits = jnp.sum(many.reshape(ni, nt, chans) * same_j[None], axis=1)
    e = jnp.exp(logits)
    e_own[...] = e
    my_rows = pl.ds(pl.multiple_of(b * ni, ni), ni)
    e_all[c, my_rows, :] = e.astype(bf16)

    pl.semaphore_wait(barrier, nc * nb - 1)

    def x_copy(k):
        c2 = lax.rem(c + k, nc)
        return pltpu.make_async_remote_copy(
            src_ref=x_all.at[c], dst_ref=x_all.at[c],
            send_sem=xs_sem.at[k], recv_sem=xr_sem.at[c],
            device_id=(c2, b), device_id_type=MESH,
        )

    loop(nc - 1, lambda k: x_copy(k + 1).start())

    half = nb // 2
    twin = b + 1 - 2 * lax.rem(b, 2)

    def e_copy(k, first, slot, own=False, across=True):
        c2 = lax.rem(c + lax.div(k, half), nc)
        b2 = lax.rem(first + 2 * lax.rem(k, half), nb)
        c3, b3 = (c, b) if own else (c2, b2)
        block = e_all.at[c3, pl.ds(pl.multiple_of(b3 * ni, ni), ni)]
        return pltpu.make_async_remote_copy(
            src_ref=block, dst_ref=block, send_sem=es_sem.at[slot],
            recv_sem=er_sem.at[c3 * nb + b3],
            device_id=(c2, b2) if across else (c, twin), device_id_type=MESH,
        )

    def e_start(k, _):
        e_copy(k, b, k, own=True).start()
        return 0

    def e_relay(k, _):
        e_copy(k, b, nc * half + k).wait_recv()
        e_copy(k, b, nc * half + k, across=False).start()
        return 0

    lax.fori_loop(1, nc * half, e_start, 0)
    e_copy(0, b, nc * half, across=False).start()

    for load in loads[6:]:
        load.wait()
    wvg[:depth, :chans] = wv_ref[...]
    wvg[:depth, chans:] = wg_ref[...]
    wvg[depth:, :] = jnp.zeros((depth, 2 * chans), bf16)
    wop[:depth, :] = jnp.zeros((depth, chans), bf16)
    wop[depth:, :] = wo_ref[...]

    head_of = lax.div(lax.broadcasted_iota(jnp.int32, (nt, LANES), 1), hd)
    head_masks = [(head_of == h).astype(f32).astype(bf16) for h in range(per)]

    def chunk(k):
        c2 = lax.rem(c + k, nc)
        if not (isinstance(k, int) and k == 0):
            block = x_all.at[c2]
            pltpu.make_async_remote_copy(
                src_ref=block, dst_ref=block, send_sem=xs_sem.at[k], recv_sem=xr_sem.at[c2],
                device_id=(c2, b), device_id_type=MESH,
            ).wait_recv()
        x = x_all[c2]
        both = dot(x, wvg[...])
        values = both[:, :chans].astype(bf16)
        gate = 1.0 / (1.0 + jnp.exp(-both[:, chans:]))
        dg = dot(x, wop[...])
        dav = (gate * dg).astype(bf16)
        if isinstance(k, int) and k == 0:
            gate_s[...] = gate
            dg_s[...] = dg
        rows = pl.ds(pl.multiple_of(c2 * nt, nt), nt)
        for s in range(ns):
            for t in range(tiles):
                cut = (slice(s * nt, (s + 1) * nt), slice(t * LANES, (t + 1) * LANES))
                da[t, rows, s * LANES:(s + 1) * LANES] = dav[cut]
                piece = values[cut]
                for h in range(per):
                    bd[c2, t, h * nt:(h + 1) * nt, s * LANES:(s + 1) * LANES] = piece * head_masks[h]

    chunk(0)
    loop(nc - 1, lambda k: chunk(k + 1))

    lax.fori_loop(1, nc * half, e_relay, 0)

    def grads(k):
        c2 = lax.rem(c + k, nc)
        for t in range(tiles):
            dw_s[c2, :, t * LANES:(t + 1) * LANES] = dot_nt(da[t], bd[c2, t])

    loop(nc, grads)

    def e_wait(k, _):
        e_copy(k, twin, nc * half).wait_recv()
        return 0

    lax.fori_loop(0, nc * half, e_wait, 0)

    group = (
        lax.div(lax.broadcasted_iota(jnp.int32, (LANES, LANES), 1), hd)
        == lax.div(lax.broadcasted_iota(jnp.int32, (LANES, LANES), 0), hd)
    ).astype(f32).astype(bf16)
    for t in range(tiles):
        lanes = slice(t * LANES, (t + 1) * LANES)

        def term(c2):
            grad = dw_s[c2, :, lanes]
            weight = e_all[c2, :, lanes].astype(f32)
            return weight * grad, weight

        dot_sum, e_sum = term(c)

        def more(k, carry):
            x, y = term(lax.rem(c + k, nc))
            return carry[0] + x, carry[1] + y

        if nc <= 4:
            for k in range(1, nc):
                dot_sum, e_sum = more(k, (dot_sum, e_sum))
        else:
            dot_sum, e_sum = lax.fori_loop(1, nc, more, (dot_sum, e_sum))
        inverse = 1.0 / split_dot(e_sum, group)
        inv_t[:, lanes] = inverse
        diff = dw_s[c, :, lanes] - split_dot(dot_sum, group) * inverse
        d_send[:, :, lanes] = diff.astype(bf16).reshape(nb, ni, LANES)

    def d_copy(k, send):
        b2 = lax.rem(b + k, nb)
        return pltpu.make_async_remote_copy(
            src_ref=d_send.at[b2], dst_ref=d_recv.at[b if send else b2],
            send_sem=ds_sem.at[k], recv_sem=dr_sem.at[b if send else b2],
            device_id=(c, b2), device_id_type=MESH,
        )

    loop(nb - 1, lambda k: d_copy(k + 1, True).start())

    tokens = pl.ds(pl.multiple_of(c * nt, nt), nt)
    for t in range(tiles):
        lanes = slice(t * LANES, (t + 1) * LANES)
        scale = inv_t[tokens, lanes]

        def add(k, total):
            return total + dot(e_all[k, tokens, lanes], bd[k, t])

        total = jnp.zeros((nt, ns * LANES), f32)
        if nc <= 4:
            for k in range(nc):
                total = add(k, total)
        else:
            total = lax.fori_loop(0, nc, add, total)
        weight = (e_all[c, :, lanes].astype(f32) * inv_t[:, lanes]).astype(bf16)
        back = dot_tn(weight, da[t])
        for s in range(ns):
            span = slice(s * LANES, (s + 1) * LANES)
            avg_s[s * nt:(s + 1) * nt, lanes] = total[:, span] * scale
            picked = back[:nt, span]
            for h in range(1, per):
                picked = jnp.where(head_of == h, back[h * nt:(h + 1) * nt, span], picked)
            dv_s[s * nt:(s + 1) * nt, lanes] = picked.astype(bf16)
    gate = gate_s[...]
    gated = gate * avg_s[...]
    res_ref[...] = dot_nt(gated.astype(bf16), wo_ref[...]).astype(bf16)
    d_pre = dg_s[...] * gated * (1.0 - gate)
    d_low = dot_nt(dv_s[...], wv_ref[...]) + dot_nt(d_pre.astype(bf16), wg_ref[...])
    dmsa_ref[...] = rows_backward(d_low, hat_s[...], rinv_s[...], mgain).astype(bf16)

    coeff = e_own[...] * inv_t[my_rows, :]
    total = d_send[b].astype(f32)
    for k in range(1, nb):
        d_copy(k, False).wait_recv()
        total = total + d_recv[lax.rem(b + k, nb)].astype(f32)
    d_logits = coeff * total
    wide = (d_logits[:, None, :] * same_j[None]).astype(bf16).reshape(ni * nt, chans)
    d_pair = dot_nt(wide, rep[...])
    dpair_ref[...] = rows_backward(d_pair, phat_s[...], prinv_s[...], pgain).astype(bf16)

    loop(nc - 1, lambda k: x_copy(k + 1).wait_send())

    def e_sent(k, _):
        e_copy(k, b, k, own=True).wait_send()
        e_copy(k, b, nc * half + k, across=False).wait_send()
        return 0

    e_copy(0, b, nc * half, across=False).wait_send()
    lax.fori_loop(1, nc * half, e_sent, 0)
    loop(nb - 1, lambda k: d_copy(k + 1, True).wait_send())


def put_out(*refs):
    sems = refs[-1]
    copies = [pltpu.make_async_copy(refs[k], refs[k + 3], sems.at[k]) for k in range(3)]
    for copy in copies:
        copy.start()
    for copy in copies:
        copy.wait()


def per_device(nc, nb, msa, pair, mgain, pgain, wv, wg, att, wo, cot):
    ns, nt, depth = msa.shape
    ni, nj, cz = pair.shape
    chans = wv.shape[1]
    nh = att.shape[1]
    tiles = chans // LANES
    n = nc * nt
    assert chans // nh == nt == nj and n == nb * ni and 2 * depth == LANES == cz
    rows = ns * nt
    vmem = pl.BlockSpec(memory_space=pltpu.VMEM)
    dma = pltpu.SemaphoreType.DMA
    outs = pl.pallas_call(
        functools.partial(kernel, nc, nb, ns, nt, ni, nh),
        out_shape=(
            pltpu.VMEM((rows, depth), bf16),
            pltpu.VMEM((rows, depth), bf16),
            pltpu.VMEM((ni * nj, cz), bf16),
        ),
        in_specs=[pl.BlockSpec(memory_space=pltpu.HBM)] * 9,
        out_specs=(vmem,) * 3,
        scratch_shapes=[
            pltpu.VMEM((nc, rows, LANES), bf16),
            pltpu.VMEM((nc, n, chans), bf16),
            pltpu.VMEM((nc, tiles, LANES, ns * LANES), bf16),
            pltpu.VMEM((tiles, n, ns * LANES), bf16),
            pltpu.VMEM((rows, chans), f32),
            pltpu.VMEM((rows, chans), f32),
            pltpu.VMEM((nc, n, chans), f32),
            pltpu.VMEM((n, chans), f32),
            pltpu.VMEM((rows, chans), f32),
            pltpu.VMEM((rows, chans), bf16),
            pltpu.VMEM((rows, depth), f32),
            pltpu.VMEM((rows, 1), f32),
            pltpu.VMEM((ni * nj, cz), f32),
            pltpu.VMEM((ni * nj, 1), f32),
            pltpu.VMEM((LANES, 2 * chans), bf16),
            pltpu.VMEM((LANES, chans), bf16),
            pltpu.VMEM((cz, chans), bf16),
            pltpu.VMEM((ni, chans), f32),
            pltpu.VMEM((nb, ni, chans), bf16),
            pltpu.VMEM((nb, ni, chans), bf16),
            pltpu.VMEM((rows, depth), bf16),
            pltpu.VMEM((ni * nj, cz), bf16),
            pltpu.VMEM((1, depth), f32),
            pltpu.VMEM((1, cz), f32),
            pltpu.VMEM(wv.shape, bf16),
            pltpu.VMEM(wg.shape, bf16),
            pltpu.VMEM((nh, cz), bf16),
            pltpu.VMEM((depth, chans), bf16),
            pltpu.VMEM((rows, depth), bf16),
            dma((nc,)), dma((nc,)), dma((nc * nb,)), dma((nc * nb,)), dma((nb,)), dma((nb,)),
            dma((9,)),
        ],
        compiler_params=pltpu.CompilerParams(
            collective_id=0, has_side_effects=True, vmem_limit_bytes=62 * 1024 * 1024
        ),
    )(
        msa.reshape(rows, depth), pair.reshape(ni * nj, cz),
        mgain.reshape(1, depth), pgain.reshape(1, cz), wv, wg, att.T, wo.T,
        cot.reshape(rows, depth),
    )
    outs = pl.pallas_call(
        put_out,
        out_shape=tuple(jax.ShapeDtypeStruct(o.shape, o.dtype) for o in outs),
        in_specs=[vmem] * 3,
        out_specs=(pl.BlockSpec(memory_space=pltpu.HBM),) * 3,
        scratch_shapes=[dma((3,))],
        compiler_params=pltpu.CompilerParams(vmem_limit_bytes=4 * 1024 * 1024),
    )(*outs)
    return outs[0].reshape(msa.shape), outs[1].reshape(msa.shape), outs[2].reshape(pair.shape)


def solution(mesh):
    block = P("bulk", "col", None)
    return jax.shard_map(
        functools.partial(per_device, mesh.shape["col"], mesh.shape["bulk"]),
        mesh=mesh,
        in_specs=(block, block, P(), P(), P(), P(), P(), P(), block),
        out_specs=(block, block, block),
        check_vma=False,
    )
```
